256 devices in a mesh: scen: 32 (over z, y), tile: 8 (over x, core).
Axes of the slice: x: 4, y: 4, z: 8, core: 2. Of those that a mesh axis runs over, the one named last changes fastest.
Arguments:
- factor_inv: bfloat16 [256, 768, 768], P('scen'), may hold values from -0.21875 to 0.21875
- pattern: int32 [256, 6, 6], P('scen'), may hold values 0 or 1
- border: bfloat16 [256, 768, 1024], P('scen', None, 'tile'), may hold values from -0.59765625 to 0.59765625
- row_scale: float32 [256, 768], P('scen'), may hold values from 0.25 to 4
- link_ids: int32 [256, 8], P('scen'), may hold values from 0 to 63, as said below
- first_diag: float32 [8192], replicated, may hold values from 10 to 100
Outputs:
- schur: float32 [8192, 8192], P('tile', 'scen')
The draws below stay inside these ranges and needn't reach their ends.
Inputs may be any that keep to these rules, and one draw needn't show every extreme that they name: link_ids[s, j] lies in group j, that is among blocks j * 8 to (j + 1) * 8 - 1. For each aligned block of 8 scenarios and each group, at most 3 of those scenarios link to one run of 2 blocks starting at a multiple of 2, and one such run has exactly 3.
All inputs are finite; a program needn't handle non-finite values. No bound on the sum of `pattern` on one device may be relied on, other than what follows from the above.
Results may differ from the reference program's by a relative error of at most 0.003.
Values may be sent and summed in bfloat16 or wider, within the bound.
No kernel may reach another device: no remote copies, remote signals or barrier semaphores. Data moves between devices by JAX's collectives and lax.ppermute only.
A program may use at most 128 MiB of HBM per device.

```python
import math
import jax
import jax.numpy as jnp
from jax import lax

BS = 128
NBLK = 6
SROWS = 768
ORDER = 8192
SC_DEV = 8
SCEN = 256
GROUPS = 8
GROUP_BLK = 8
OWN_BLK = 2
OPG = 4
CAP = 3
N_SCEN = 32


def draw_link_ids(key, part):
    key_heavy, key_offset, key_order, key_sub = jax.random.split(key, 4)
    heavy_owner = jax.random.randint(key_heavy, (N_SCEN, GROUPS), 0, OPG)
    offset_draw = jax.random.randint(key_offset, (N_SCEN, GROUPS), 0, OPG - 1)
    position = jnp.arange(SC_DEV)
    rest_index = jnp.maximum(position - CAP, 0)
    other_owner = (heavy_owner[:, :, None] + 1 + (offset_draw[:, :, None] + rest_index[None, None, :]) % (OPG - 1)) % OPG
    owner_seq = jnp.where(position[None, None, :] < CAP, heavy_owner[:, :, None], other_owner)
    sort_keys = jax.random.randint(key_order, (N_SCEN, GROUPS, SC_DEV), 0, 1048576) * SC_DEV + position[None, None, :]
    order_index = jnp.argsort(sort_keys, axis=-1)
    owner_final = jnp.take_along_axis(owner_seq, order_index, axis=-1)
    sub_block = jax.random.randint(key_sub, (N_SCEN, GROUPS, SC_DEV), 0, OWN_BLK)
    group_index = jnp.arange(GROUPS)[None, :, None]
    link_block = group_index * GROUP_BLK + owner_final * OWN_BLK + sub_block
    return jnp.transpose(link_block, (0, 2, 1)).reshape(SCEN, GROUPS).astype(jnp.int32)


def plant(result, rng, smallest, high):
    place = [jax.random.randint(jax.random.fold_in(rng, axis), (), 0, length) for axis, length in enumerate(result.shape)]
    longest = result.shape.index(max(result.shape))
    beside = place[:longest] + [(place[longest] + 1) % result.shape[longest]] + place[longest + 1:]
    return result.at[tuple(place)].set(smallest).at[tuple(beside)].set(high)


def steps_of(key, extent, cuts, low, largest):
    def one(dim, blocks):
        draws = jax.random.uniform(jax.random.fold_in(jax.random.fold_in(key, 6), dim), (blocks,), jnp.float32, low / len(cuts), largest / len(cuts))
        return jnp.repeat(jnp.exp(draws), extent[dim] // blocks).reshape((-1,) + (1,) * (len(extent) - dim - 1))

    gain = one(*cuts[0])
    for cut in cuts[1:]:
        gain = gain * one(*cut)
    return gain


def gaussian(stream_key, extent, scale, most, cuts=(), kind=jnp.bfloat16):
    result = jax.random.normal(stream_key, extent, jnp.float32) * scale
    if len(cuts) > 0:
        result = steps_of(stream_key, extent, cuts, -0.22, 0.18) * result
    return jnp.clip(result, min=-most, max=most).astype(kind)


def setup_inputs(seed: int = 0) -> dict:
    keys = jax.random.split(jax.random.key(seed), 7)
    return {
        "factor_inv": gaussian(keys[0], (SCEN, SROWS, SROWS), SROWS ** -0.5, 0.21875, ((0, 32),)),
        "pattern": plant((jax.random.randint(keys[1], (SCEN, NBLK, NBLK), 0, 2) < 1).astype(jnp.int32), jax.random.fold_in(keys[1], 1), 0, 1),
        "border": gaussian(keys[2], (SCEN, SROWS, GROUPS * BS), 0.1, 0.59765625, ((0, 32), (2, 8))),
        "row_scale": jnp.clip(jnp.exp(math.log(4.0) - 2.7725887 * jax.random.uniform(keys[3], (SCEN, SROWS), jnp.float32) ** steps_of(keys[3], (SCEN, SROWS), ((0, 32),), -0.2, 0.2)), 0.25, 4.0),
        "link_ids": draw_link_ids(jax.random.fold_in(keys[6], 71), 0),
        "first_diag": jnp.clip(jnp.exp(jax.random.uniform(keys[5], (ORDER,), jnp.float32, math.log(10.0), math.log(100.0))), 10.0, 100.0),
    }


def reference(factor_inv, pattern, border, row_scale, link_ids, first_diag):
    index_blocks = jnp.arange(NBLK)
    diagonal_mask = (index_blocks[:, None] == index_blocks[None, :]).astype(jnp.int32)
    below_diag = (index_blocks[:, None] > index_blocks[None, :]).astype(jnp.int32)

    def add_scenario(schur_sum, inputs):
        finv, pat, bord, scale_rows, link_list = inputs
        effective = jnp.where(diagonal_mask == 1, 1, pat * below_diag)
        expanded = jnp.repeat(jnp.repeat(effective, BS, axis=0), BS, axis=1).astype(jnp.bfloat16)
        masked = finv * expanded
        solved = jnp.dot(masked, bord, preferred_element_type=jnp.float32).astype(jnp.bfloat16)
        scaled = (scale_rows[:, None] * solved.astype(jnp.float32)).astype(jnp.bfloat16)
        schur_block = jnp.dot(scaled.T, solved, preferred_element_type=jnp.float32)
        row_index = (link_list[:, None] * BS + jnp.arange(BS)[None, :]).reshape(-1).astype(jnp.int32)
        schur_sum = schur_sum.at[row_index[:, None], row_index[None, :]].add(schur_block)
        return schur_sum, None

    start_sum = jnp.zeros((ORDER, ORDER), jnp.float32)
    schur_sum = lax.scan(add_scenario, start_sum, (factor_inv, pattern, border, row_scale, link_ids))[0]
    diag_index = jnp.arange(ORDER)
    return schur_sum.at[diag_index, diag_index].add(first_diag)
```

```python
import jax
import jax.numpy as jnp
from jax import lax
from jax.experimental import pallas as pl
from jax.experimental.pallas import tpu as pltpu
from jax.sharding import Mesh, PartitionSpec as P

BF = jnp.bfloat16
F32 = jnp.float32


def pair_kernel(tile_ref, pattern_ref, factor_ref, border_ref, scale_ref, out_ref, solved_ref, scaled_ref):
    groups, rows, bs = border_ref.shape
    nblk = rows // bs
    tile = tile_ref[0]
    for a in range(nblk):
        lo, hi = a * bs, (a + 1) * bs
        parts = []
        for b in range(a + 1):
            block = factor_ref[0, lo:hi, b * bs:(b + 1) * bs]
            if b < a:
                keep = pattern_ref[tile, a * nblk + b] != 0
                block = jnp.where(keep, block, jnp.zeros_like(block))
            parts.append(block)
        masked = jnp.concatenate(parts, axis=1)
        scale = scale_ref[lo:hi, :]
        for g in range(0, groups, 2):
            rhs = jnp.concatenate([border_ref[g, :hi, :], border_ref[g + 1, :hi, :]], axis=1)
            solved = jnp.dot(masked, rhs, preferred_element_type=F32).astype(BF)
            solved_ref[lo:hi, g * bs:(g + 2) * bs] = solved
            scaled_ref[lo:hi, g * bs:(g + 2) * bs] = (scale * solved.astype(F32)).astype(BF)
    for i in range(0, groups, 2):
        lhs = scaled_ref[:, i * bs:(i + 2) * bs]
        for j in range(0, groups, 2):
            rhs = solved_ref[:, j * bs:(j + 2) * bs]
            pair = lax.dot_general(
                lhs, rhs, (((0,), (0,)), ((), ())), preferred_element_type=F32
            ).astype(BF)
            for di in range(2):
                for dj in range(2):
                    out_ref[(j + dj) * groups + i + di] = pair[
                        di * bs:(di + 1) * bs, dj * bs:(dj + 1) * bs
                    ]


def bin_kernel(target_ref, blocks_ref, out_ref, acc_ref):
    acc_ref[...] = jnp.zeros_like(acc_ref)

    def add(k, carry):
        t = target_ref[k]
        acc_ref[t] += blocks_ref[k].astype(F32)
        return carry

    lax.fori_loop(0, blocks_ref.shape[0], add, 0)
    out_ref[...] = acc_ref[...].astype(BF)


def final_kernel(where_ref, parts_ref, diag_ref, out_ref):
    sources, _, bs, _ = parts_ref.shape
    row_blocks = out_ref.shape[0] // bs
    col_blocks = out_ref.shape[1] // bs
    first_row = where_ref[0]
    first_col = where_ref[1]
    eye = lax.broadcasted_iota(jnp.int32, (bs, bs), 0) == lax.broadcasted_iota(jnp.int32, (bs, bs), 1)
    for r in range(row_blocks):
        for c in range(col_blocks):
            total = parts_ref[0, r * col_blocks + c].astype(F32)
            for s in range(1, sources):
                total = total + parts_ref[s, r * col_blocks + c].astype(F32)
            diag = diag_ref[pl.ds(first_row + r, 1), :]
            on = jnp.logical_and(eye, first_row + r == first_col + c)
            total = total + jnp.where(on, jnp.broadcast_to(diag, (bs, bs)), 0.0)
            out_ref[r * bs:(r + 1) * bs, c * bs:(c + 1) * bs] = total


VMEM = pl.BlockSpec(memory_space=pltpu.VMEM)
SMEM = pl.BlockSpec(memory_space=pltpu.SMEM)


def on_device(factor_inv, pattern, border, row_scale, link_ids, first_diag):
    local_scen, rows, _ = factor_inv.shape
    nblk = pattern.shape[1]
    bs = border.shape[2]
    groups = link_ids.shape[1]
    tile = lax.axis_index(("x", "core"))
    z = lax.axis_index("z")
    y = lax.axis_index("y")
    y_count = lax.axis_size("y")
    order_blocks = first_diag.shape[0] // bs
    group_blocks = order_blocks // groups
    own_cols = group_blocks // y_count

    links = lax.all_gather(link_ids, "z", axis=0, tiled=True)
    borders = lax.all_to_all(border, ("x", "core"), 0, 0, tiled=True)

    scale = lax.dynamic_slice_in_dim(row_scale, tile, 1, 0).reshape(rows, 1)
    pairs = pl.pallas_call(
        pair_kernel,
        out_shape=jax.ShapeDtypeStruct((groups * groups, bs, bs), BF),
        grid_spec=pltpu.PrefetchScalarGridSpec(
            num_scalar_prefetch=2,
            grid=(1,),
            in_specs=[
                pl.BlockSpec((1, rows, rows), lambda i, t, p: (t[0], 0, 0)),
                pl.BlockSpec((groups, rows, bs), lambda i, t, p: (0, 0, 0)),
                pl.BlockSpec((rows, 1), lambda i, t, p: (0, 0)),
            ],
            out_specs=pl.BlockSpec((groups * groups, bs, bs), lambda i, t, p: (0, 0, 0)),
            scratch_shapes=[pltpu.VMEM((rows, groups * bs), BF), pltpu.VMEM((rows, groups * bs), BF)],
        ),
        compiler_params=pltpu.CompilerParams(vmem_limit_bytes=40 << 20),
        name="pair",
    )(tile.reshape(1), pattern.reshape(local_scen, nblk * nblk), factor_inv, borders, scale)

    received = lax.all_to_all(pairs, ("z", "x", "core"), 0, 0, tiled=True)

    row_bin = lax.dynamic_slice_in_dim(links, tile, 1, 1)[:, 0] - tile * group_blocks
    col_bin = lax.dynamic_slice_in_dim(links, z, 1, 1)[:, 0] - z * group_blocks
    target = (col_bin // own_cols) * (group_blocks * own_cols) + row_bin * own_cols + col_bin % own_cols
    bins = pl.pallas_call(
        bin_kernel,
        out_shape=jax.ShapeDtypeStruct((group_blocks * group_blocks, bs, bs), BF),
        in_specs=[SMEM, VMEM],
        out_specs=VMEM,
        scratch_shapes=[pltpu.VMEM((group_blocks * group_blocks, bs, bs), F32)],
        compiler_params=pltpu.CompilerParams(vmem_limit_bytes=40 << 20),
        name="bins",
    )(target, received)

    parts = lax.all_to_all(
        bins.reshape(y_count, group_blocks * own_cols, bs, bs), "y", 0, 0, tiled=True
    )
    place = jnp.stack([tile * group_blocks, z * group_blocks + y * own_cols])
    return pl.pallas_call(
        final_kernel,
        out_shape=jax.ShapeDtypeStruct((group_blocks * bs, own_cols * bs), F32),
        in_specs=[SMEM, VMEM, VMEM],
        out_specs=VMEM,
        compiler_params=pltpu.CompilerParams(vmem_limit_bytes=40 << 20),
        name="final",
    )(place, parts, first_diag.reshape(order_blocks, bs))


def solution(mesh):
    chips = Mesh(mesh.devices.reshape(8, 4, 4, 2), ("z", "y", "x", "core"))
    scen, tile = ("z", "y"), ("x", "core")
    in_specs = (
        P(scen, None, None),
        P(scen, None, None),
        P(scen, None, tile),
        P(scen, None),
        P(scen, None),
        P(),
    )
    return jax.shard_map(
        on_device, mesh=chips, in_specs=in_specs, out_specs=P(tile, scen), check_vma=False
    )
```

```python
import jax
import jax.numpy as jnp
from jax import lax
from jax.experimental import pallas as pl
from jax.experimental.pallas import tpu as pltpu
from jax.sharding import Mesh, PartitionSpec as P

BF = jnp.bfloat16
F32 = jnp.float32
TAG = 8

VMEM = pl.BlockSpec(memory_space=pltpu.VMEM)
SMEM = pl.BlockSpec(memory_space=pltpu.SMEM)
HBM = pl.BlockSpec(memory_space=pltpu.HBM)
PARAMS = pltpu.CompilerParams(vmem_limit_bytes=32 << 20)
WIDE = pltpu.CompilerParams(vmem_limit_bytes=60 << 20)


def mask_kernel(tile_ref, pattern_ref, factor_hbm, out_ref, buf_ref, sems):
    rows = buf_ref.shape[0]
    nblk = sems.shape[0]
    bs = rows // nblk
    tile = tile_ref[0]
    copies = [
        pltpu.make_async_copy(
            factor_hbm.at[tile, pl.ds(a * bs, bs), :], buf_ref.at[pl.ds(a * bs, bs), :], sems.at[a]
        )
        for a in range(nblk)
    ]
    for copy in copies:
        copy.start()
    for a in range(nblk):
        copies[a].wait()
        lo, hi = a * bs, (a + 1) * bs
        for b in range(nblk):
            block = buf_ref[lo:hi, b * bs:(b + 1) * bs]
            if b < a:
                keep = pattern_ref[tile, a * nblk + b] != 0
                block = jnp.where(keep, block, jnp.zeros_like(block))
            if b > a:
                block = jnp.zeros_like(block)
            out_ref[lo:hi, b * bs:(b + 1) * bs] = block


def pair_kernel(shift_ref, link_ref, masked_ref, border_ref, scale_ref, out_ref, solved_ref, scaled_ref):
    groups, rows, bs = border_ref.shape
    tile, own_cols, bins_y, group_blocks = (shift_ref[k] for k in range(4))
    for g in range(0, groups, 2):
        rhs = jnp.concatenate([border_ref[g], border_ref[g + 1]], axis=1)
        for a in range(0, rows, 2 * bs):
            lo, hi = a, a + 2 * bs
            solved = jnp.dot(
                masked_ref[lo:hi, :hi], rhs[:hi], preferred_element_type=F32
            ).astype(BF)
            solved_ref[lo:hi, g * bs:(g + 2) * bs] = solved
            scaled_ref[lo:hi, g * bs:(g + 2) * bs] = (
                scale_ref[lo:hi, :] * solved.astype(F32)
            ).astype(BF)
    for i in range(groups):
        row_bin = link_ref[tile, i] - i * group_blocks
        for j in range(groups):
            col_bin = link_ref[tile, j] - j * group_blocks
            owner = lax.div(col_bin, own_cols)
            target = owner * bins_y + row_bin * own_cols + (col_bin - owner * own_cols)
            out_ref[i * groups + j, bs:, :] = jnp.full((TAG, bs), target.astype(F32)).astype(BF)
    for i in range(0, groups, 2):
        lhs = scaled_ref[:, i * bs:(i + 2) * bs]
        for j in range(0, groups, 2):
            rhs = solved_ref[:, j * bs:(j + 2) * bs]
            pair = lax.dot_general(
                lhs, rhs, (((0,), (0,)), ((), ())), preferred_element_type=F32
            ).astype(BF)
            for di in range(2):
                for dj in range(2):
                    out_ref[(i + di) * groups + j + dj, :bs, :] = pair[
                        di * bs:(di + 1) * bs, dj * bs:(dj + 1) * bs
                    ]


def bin_kernel(blocks_hbm, out_hbm, acc_ref, tag_ref, in_ref, buf_ref, meta_ref, target_ref, in_sems, out_sems):
    chunks = in_sems.shape[0] - 2
    count, bs, _ = in_ref.shape
    size = count // chunks
    tags = pltpu.make_async_copy(blocks_hbm.at[:, pl.ds(bs, TAG), :], tag_ref, in_sems.at[chunks])
    tags.start()
    loads = [
        pltpu.make_async_copy(
            blocks_hbm.at[pl.ds(c * size, size), pl.ds(0, bs), :],
            in_ref.at[pl.ds(c * size, size)],
            in_sems.at[c],
        )
        for c in range(chunks)
    ]
    for load in loads:
        load.start()
    tags.wait()
    lane = lax.broadcasted_iota(jnp.int32, (TAG, bs), 1)
    meta = jnp.zeros((TAG, bs), F32)
    for k in range(count):
        meta = jnp.where(lane == k, tag_ref[k].astype(F32), meta)
    meta_ref[...] = meta.astype(jnp.int32)
    targets = pltpu.make_async_copy(meta_ref, target_ref, in_sems.at[chunks + 1])
    targets.start()
    acc_ref[...] = jnp.zeros_like(acc_ref)
    targets.wait()
    for c in range(chunks):
        loads[c].wait()
        for k in range(c * size, (c + 1) * size):
            acc_ref[target_ref[0, k]] += in_ref[k].astype(F32)
    parts, per = buf_ref.shape[:2]
    stores = []
    for p in range(parts):
        buf_ref[p] = acc_ref[p * per:(p + 1) * per].astype(BF)
        store = pltpu.make_async_copy(buf_ref.at[p], out_hbm.at[p], out_sems.at[p])
        store.start()
        stores.append(store)
    for store in stores:
        store.wait()


def final_kernel(where_ref, diag_ref, *rest):
    parts_refs, out_ref = rest[:-1], rest[-1]
    sources, _, _, bs = parts_refs[0].shape
    row_blocks = out_ref.shape[0] // bs
    col_blocks = out_ref.shape[1] // bs
    first_row = where_ref[0]
    first_col = where_ref[1]
    for r in range(row_blocks):
        diag = diag_ref[pl.ds(first_row + r, 1), :]
        for c in range(col_blocks):
            here = first_row + r == first_col + c
            start = 0
            for parts_ref in parts_refs:
                size = parts_ref.shape[2]
                total = parts_ref[0, r * col_blocks + c].astype(F32)
                for s in range(1, sources):
                    total = total + parts_ref[s, r * col_blocks + c].astype(F32)
                eye = (
                    lax.broadcasted_iota(jnp.int32, (size, bs), 0) + start
                    == lax.broadcasted_iota(jnp.int32, (size, bs), 1)
                )
                on = jnp.logical_and(eye, here)
                total = total + jnp.where(on, jnp.broadcast_to(diag, (size, bs)), 0.0)
                out_ref[r * bs + start:r * bs + start + size, c * bs:(c + 1) * bs] = total
                start += size


def on_device(factor_inv, pattern, border, row_scale, link_ids, first_diag):
    local_scen, rows, _ = factor_inv.shape
    nblk = pattern.shape[1]
    bs = border.shape[2]
    groups = link_ids.shape[1]
    tile = lax.axis_index(("x", "core"))
    z = lax.axis_index("z")
    y = lax.axis_index("y")
    y_count = lax.axis_size("y")
    order_blocks = first_diag.shape[0] // bs
    group_blocks = order_blocks // groups
    own_cols = group_blocks // y_count
    bins_y = group_blocks * own_cols

    borders = lax.all_to_all(border, ("x", "core"), 0, 0, tiled=True)

    masked = pl.pallas_call(
        mask_kernel,
        out_shape=jax.ShapeDtypeStruct((rows, rows), BF),
        in_specs=[SMEM, SMEM, HBM],
        out_specs=VMEM,
        scratch_shapes=[pltpu.VMEM((rows, rows), BF), pltpu.SemaphoreType.DMA((nblk,))],
        compiler_params=PARAMS,
        name="mask",
    )(tile.reshape(1), pattern.reshape(local_scen, nblk * nblk), factor_inv)
    scale = lax.dynamic_slice_in_dim(row_scale, tile, 1, 0).reshape(rows, 1)
    shift = jnp.stack([tile, jnp.int32(own_cols), jnp.int32(bins_y), jnp.int32(group_blocks)])
    pairs = pl.pallas_call(
        pair_kernel,
        out_shape=jax.ShapeDtypeStruct((groups * groups, bs + TAG, bs), BF),
        in_specs=[SMEM, SMEM, VMEM, VMEM, VMEM],
        out_specs=VMEM,
        scratch_shapes=[pltpu.VMEM((rows, groups * bs), BF) for _ in range(2)],
        compiler_params=PARAMS,
        name="pair",
    )(shift, link_ids, masked, borders, scale)
    received = lax.all_to_all(pairs, ("x", "core", "z"), 0, 0, tiled=True)
    bins = pl.pallas_call(
        bin_kernel,
        out_shape=jax.ShapeDtypeStruct((y_count, bins_y, bs, bs), BF),
        in_specs=[HBM],
        out_specs=HBM,
        scratch_shapes=[
            pltpu.VMEM((y_count * bins_y, bs, bs), F32),
            pltpu.VMEM((groups * local_scen, TAG, bs), BF),
            pltpu.VMEM((groups * local_scen, bs, bs), BF),
            pltpu.VMEM((y_count, bins_y, bs, bs), BF),
            pltpu.VMEM((TAG, bs), jnp.int32),
            pltpu.SMEM((TAG, bs), jnp.int32),
            pltpu.SemaphoreType.DMA((groups + 2,)),
            pltpu.SemaphoreType.DMA((y_count,)),
        ],
        compiler_params=WIDE,
        name="bins",
    )(received)
    parts = [lax.all_to_all(bins, "y", 0, 0, tiled=True)]
    place = jnp.stack([tile * group_blocks, z * group_blocks + y * own_cols])
    return pl.pallas_call(
        final_kernel,
        out_shape=jax.ShapeDtypeStruct((group_blocks * bs, own_cols * bs), F32),
        in_specs=[SMEM, VMEM] + [VMEM for _ in parts],
        out_specs=VMEM,
        compiler_params=PARAMS,
        name="final",
    )(place, first_diag.reshape(order_blocks, bs), *parts)


def solution(mesh):
    chips = Mesh(mesh.devices.reshape(8, 4, 4, 2), ("z", "y", "x", "core"))
    scen, tile = ("z", "y"), ("x", "core")
    in_specs = (
        P(scen, None, None),
        P(scen, None, None),
        P(scen, None, tile),
        P(scen, None),
        P(scen, None),
        P(),
    )
    return jax.shard_map(
        on_device, mesh=chips, in_specs=in_specs, out_specs=P(tile, scen), check_vma=False
    )
```

```python
import jax
import jax.numpy as jnp
from jax import lax
from jax.experimental import pallas as pl
from jax.experimental.pallas import tpu as pltpu
from jax.sharding import Mesh, PartitionSpec as P

BF = jnp.bfloat16
F32 = jnp.float32
TAG = 8

VMEM = pl.BlockSpec(memory_space=pltpu.VMEM)
SMEM = pl.BlockSpec(memory_space=pltpu.SMEM)
HBM = pl.BlockSpec(memory_space=pltpu.HBM)
PARAMS = pltpu.CompilerParams(vmem_limit_bytes=32 << 20)


def mask_kernel(tile_ref, pattern_ref, factor_hbm, out_ref, buf_ref, sems):
    rows = buf_ref.shape[0]
    nblk = sems.shape[0]
    bs = rows // nblk
    tile = tile_ref[0]
    copies = [
        pltpu.make_async_copy(
            factor_hbm.at[tile, pl.ds(a * bs, bs), :], buf_ref.at[pl.ds(a * bs, bs), :], sems.at[a]
        )
        for a in range(nblk)
    ]
    for copy in copies:
        copy.start()
    for a in range(nblk):
        copies[a].wait()
        lo, hi = a * bs, (a + 1) * bs
        for b in range(nblk):
            block = buf_ref[lo:hi, b * bs:(b + 1) * bs]
            if b < a:
                keep = pattern_ref[tile, a * nblk + b] != 0
                block = jnp.where(keep, block, jnp.zeros_like(block))
            if b > a:
                block = jnp.zeros_like(block)
            out_ref[lo:hi, b * bs:(b + 1) * bs] = block


def pair_kernel(shift_ref, link_ref, masked_ref, border_ref, scale_ref, out_hbm, out_ref, solved_ref, scaled_ref, sems):
    groups, rows, bs = border_ref.shape
    tile, own_cols, bins_y, group_blocks = (shift_ref[k] for k in range(4))
    for g in range(0, groups, 2):
        rhs = jnp.concatenate([border_ref[g], border_ref[g + 1]], axis=1)
        for a in range(0, rows, 2 * bs):
            lo, hi = a, a + 2 * bs
            solved = jnp.dot(
                masked_ref[lo:hi, :hi], rhs[:hi], preferred_element_type=F32
            ).astype(BF)
            solved_ref[lo:hi, g * bs:(g + 2) * bs] = solved
            scaled_ref[lo:hi, g * bs:(g + 2) * bs] = (
                scale_ref[lo:hi, :] * solved.astype(F32)
            ).astype(BF)
    for i in range(groups):
        row_bin = link_ref[tile, i] - i * group_blocks
        for j in range(groups):
            col_bin = link_ref[tile, j] - j * group_blocks
            owner = lax.div(col_bin, own_cols)
            target = owner * bins_y + row_bin * own_cols + (col_bin - owner * own_cols)
            out_ref[i * groups + j, bs:, :] = jnp.full((TAG, bs), target.astype(F32)).astype(BF)
    stores = []
    for i in range(0, groups, 2):
        lhs = scaled_ref[:, i * bs:(i + 2) * bs]
        for j in range(0, groups, 2):
            rhs = solved_ref[:, j * bs:(j + 2) * bs]
            pair = lax.dot_general(
                lhs, rhs, (((0,), (0,)), ((), ())), preferred_element_type=F32
            ).astype(BF)
            for di in range(2):
                for dj in range(2):
                    out_ref[(i + di) * groups + j + dj, :bs, :] = pair[
                        di * bs:(di + 1) * bs, dj * bs:(dj + 1) * bs
                    ]
        part = pl.ds(i * groups, 2 * groups)
        store = pltpu.make_async_copy(out_ref.at[part], out_hbm.at[part], sems.at[i // 2])
        store.start()
        stores.append(store)
    for store in stores:
        store.wait()


def bin_kernel(shift_ref, in_ref, *rest):
    own, far_a, far_b, up_b, down_a, up_a, down_b = rest[:7]
    acc_ref, meta_ref, target_ref, sem = rest[7:]
    count, bs = in_ref.shape[0], in_ref.shape[2]
    lane = lax.broadcasted_iota(jnp.int32, (TAG, bs), 1)
    meta = jnp.zeros((TAG, bs), F32)
    for k in range(count):
        meta = jnp.where(lane == k, in_ref[k, bs:, :].astype(F32), meta)
    meta_ref[...] = meta.astype(jnp.int32)
    targets = pltpu.make_async_copy(meta_ref, target_ref, sem)
    targets.start()
    acc_ref[...] = jnp.zeros_like(acc_ref)
    targets.wait()
    for k in range(count):
        acc_ref[target_ref[0, k]] += in_ref[k, :bs, :].astype(F32)
    per = own.shape[0]
    parts = acc_ref.shape[0] // per
    for hop, pieces in ((2, (far_a, far_b)), (1, (up_a, up_b)), (3, (down_a, down_b)), (0, (own,))):
        start = lax.rem(shift_ref[0] + hop, parts) * per
        size = per // len(pieces)
        for n, piece in enumerate(pieces):
            piece[...] = acc_ref[pl.ds(start + n * size, size)].astype(BF)


def final_kernel(where_ref, diag_ref, own_ref, up_a_ref, down_a_ref, up_b_ref, down_b_ref, out_ref):
    count, bs, _ = own_ref.shape
    row_blocks = out_ref.shape[0] // bs
    col_blocks = out_ref.shape[1] // bs
    half = count // 2
    first_row = where_ref[0]
    first_col = where_ref[1]
    eye = lax.broadcasted_iota(jnp.int32, (bs, bs), 0) == lax.broadcasted_iota(jnp.int32, (bs, bs), 1)
    for r in range(row_blocks):
        diag = diag_ref[pl.ds(first_row + r, 1), :]
        for c in range(col_blocks):
            n = r * col_blocks + c
            one, two = (up_a_ref, down_a_ref) if n < half else (up_b_ref, down_b_ref)
            total = own_ref[n].astype(F32) + one[n % half].astype(F32) + two[n % half].astype(F32)
            on = jnp.logical_and(eye, first_row + r == first_col + c)
            total = total + jnp.where(on, jnp.broadcast_to(diag, (bs, bs)), 0.0)
            out_ref[r * bs:(r + 1) * bs, c * bs:(c + 1) * bs] = total


def on_device(factor_inv, pattern, border, row_scale, link_ids, first_diag):
    local_scen, rows, _ = factor_inv.shape
    nblk = pattern.shape[1]
    bs = border.shape[2]
    groups = link_ids.shape[1]
    tile = lax.axis_index(("x", "core"))
    z = lax.axis_index("z")
    y = lax.axis_index("y")
    y_count = lax.axis_size("y")
    order_blocks = first_diag.shape[0] // bs
    group_blocks = order_blocks // groups
    own_cols = group_blocks // y_count
    bins_y = group_blocks * own_cols

    borders = lax.all_to_all(border, ("x", "core"), 0, 0, tiled=True)

    masked = pl.pallas_call(
        mask_kernel,
        out_shape=jax.ShapeDtypeStruct((rows, rows), BF),
        in_specs=[SMEM, SMEM, HBM],
        out_specs=VMEM,
        scratch_shapes=[pltpu.VMEM((rows, rows), BF), pltpu.SemaphoreType.DMA((nblk,))],
        compiler_params=PARAMS,
        name="mask",
    )(tile.reshape(1), pattern.reshape(local_scen, nblk * nblk), factor_inv)
    scale = lax.dynamic_slice_in_dim(row_scale, tile, 1, 0).reshape(rows, 1)
    shift = jnp.stack([tile, jnp.int32(own_cols), jnp.int32(bins_y), jnp.int32(group_blocks)])
    pairs = pl.pallas_call(
        pair_kernel,
        out_shape=jax.ShapeDtypeStruct((groups * groups, bs + TAG, bs), BF),
        in_specs=[SMEM, SMEM, VMEM, VMEM, VMEM],
        out_specs=HBM,
        scratch_shapes=[pltpu.VMEM((groups * groups, bs + TAG, bs), BF)]
        + [pltpu.VMEM((rows, groups * bs), BF) for _ in range(2)]
        + [pltpu.SemaphoreType.DMA((groups // 2,))],
        compiler_params=PARAMS,
        name="pair",
    )(shift, link_ids, masked, borders, scale)
    received = lax.all_to_all(pairs, ("x", "core", "z"), 0, 0, tiled=True)
    half = jax.ShapeDtypeStruct((bins_y // 2, bs, bs), BF)
    own, far_a, far_b, up_b, down_a, up_a, down_b = pl.pallas_call(
        bin_kernel,
        out_shape=[jax.ShapeDtypeStruct((bins_y, bs, bs), BF)] + [half] * 6,
        in_specs=[SMEM, VMEM],
        out_specs=[VMEM] * 7,
        scratch_shapes=[
            pltpu.VMEM((y_count * bins_y, bs, bs), F32),
            pltpu.VMEM((TAG, bs), jnp.int32),
            pltpu.SMEM((TAG, bs), jnp.int32),
            pltpu.SemaphoreType.DMA,
        ],
        compiler_params=PARAMS,
        name="bins",
    )(y.reshape(1), received)
    def send(value, hop):
        return lax.ppermute(value, "y", [(k, (k + hop) % y_count) for k in range(y_count)])

    def add(one, two):
        return (one.astype(F32) + two.astype(F32)).astype(BF)

    far_a, far_b = send(far_a, 1), send(far_b, -1)
    up_b, down_a = send(up_b, 1), send(down_a, -1)
    up_a, down_b = send(add(up_a, far_a), 1), send(add(down_b, far_b), -1)
    place = jnp.stack([tile * group_blocks, z * group_blocks + y * own_cols])
    return pl.pallas_call(
        final_kernel,
        out_shape=jax.ShapeDtypeStruct((group_blocks * bs, own_cols * bs), F32),
        in_specs=[SMEM] + [VMEM] * 6,
        out_specs=VMEM,
        compiler_params=PARAMS,
        name="final",
    )(place, first_diag.reshape(order_blocks, bs), own, up_a, down_a, up_b, down_b)


def solution(mesh):
    chips = Mesh(mesh.devices.reshape(8, 4, 4, 2), ("z", "y", "x", "core"))
    scen, tile = ("z", "y"), ("x", "core")
    in_specs = (
        P(scen, None, None),
        P(scen, None, None),
        P(scen, None, tile),
        P(scen, None),
        P(scen, None),
        P(),
    )
    return jax.shard_map(
        on_device, mesh=chips, in_specs=in_specs, out_specs=P(tile, scen), check_vma=False
    )
```

```python
import jax
import jax.numpy as jnp
from jax import lax
from jax.experimental import pallas as pl
from jax.experimental.pallas import tpu as pltpu
from jax.sharding import Mesh, PartitionSpec as P

BF = jnp.bfloat16
F32 = jnp.float32

VMEM = pl.BlockSpec(memory_space=pltpu.VMEM)
SMEM = pl.BlockSpec(memory_space=pltpu.SMEM)
HBM = pl.BlockSpec(memory_space=pltpu.HBM)
PARAMS = pltpu.CompilerParams(vmem_limit_bytes=32 << 20)


def mask_kernel(tile_ref, pattern_ref, factor_hbm, out_ref, buf_ref, sems):
    rows = buf_ref.shape[0]
    nblk = sems.shape[0]
    bs = rows // nblk
    tile = tile_ref[0]
    copies = [
        pltpu.make_async_copy(
            factor_hbm.at[tile, pl.ds(a * bs, bs), :], buf_ref.at[pl.ds(a * bs, bs), :], sems.at[a]
        )
        for a in range(nblk)
    ]
    for copy in copies:
        copy.start()
    for a in range(nblk):
        copies[a].wait()
        lo, hi = a * bs, (a + 1) * bs
        for b in range(nblk):
            block = buf_ref[lo:hi, b * bs:(b + 1) * bs]
            if b < a:
                keep = pattern_ref[tile, a * nblk + b] != 0
                block = jnp.where(keep, block, jnp.zeros_like(block))
            if b > a:
                block = jnp.zeros_like(block)
            out_ref[lo:hi, b * bs:(b + 1) * bs] = block


def pair_kernel(masked_ref, border_ref, scale_ref, out_ref, solved_ref, scaled_ref):
    groups, rows, bs = border_ref.shape
    for g in range(0, groups, 2):
        rhs = jnp.concatenate([border_ref[g], border_ref[g + 1]], axis=1)
        for a in range(0, rows, 2 * bs):
            lo, hi = a, a + 2 * bs
            solved = jnp.dot(
                masked_ref[lo:hi, :hi], rhs[:hi], preferred_element_type=F32
            ).astype(BF)
            solved_ref[lo:hi, g * bs:(g + 2) * bs] = solved
            scaled_ref[lo:hi, g * bs:(g + 2) * bs] = (
                scale_ref[lo:hi, :] * solved.astype(F32)
            ).astype(BF)
    for i in range(0, groups, 2):
        lhs = scaled_ref[:, i * bs:(i + 2) * bs]
        for j in range(0, groups, 2):
            rhs = solved_ref[:, j * bs:(j + 2) * bs]
            pair = lax.dot_general(
                lhs, rhs, (((0,), (0,)), ((), ())), preferred_element_type=F32
            ).astype(BF)
            for di in range(2):
                for dj in range(2):
                    out_ref[(i + di) * groups + j + dj] = pair[
                        di * bs:(di + 1) * bs, dj * bs:(dj + 1) * bs
                    ]


def bin_kernel(shift_ref, target_ref, in_ref, *rest):
    own, far_a, far_b, up_b, down_a, up_a, down_b = rest[:7]
    acc_ref = rest[7]
    acc_ref[...] = jnp.zeros_like(acc_ref)
    for k in range(in_ref.shape[0]):
        acc_ref[target_ref[k]] += in_ref[k].astype(F32)
    per = own.shape[0]
    parts = acc_ref.shape[0] // per
    for hop, pieces in ((2, (far_a, far_b)), (1, (up_a, up_b)), (3, (down_a, down_b)), (0, (own,))):
        start = lax.rem(shift_ref[0] + hop, parts) * per
        size = per // len(pieces)
        for n, piece in enumerate(pieces):
            piece[...] = acc_ref[pl.ds(start + n * size, size)].astype(BF)


def final_kernel(where_ref, diag_ref, own_ref, up_a_ref, down_a_ref, up_b_ref, down_b_ref, out_ref):
    count, bs, _ = own_ref.shape
    row_blocks = out_ref.shape[0] // bs
    col_blocks = out_ref.shape[1] // bs
    half = count // 2
    first_row = where_ref[0]
    first_col = where_ref[1]
    eye = lax.broadcasted_iota(jnp.int32, (bs, bs), 0) == lax.broadcasted_iota(jnp.int32, (bs, bs), 1)
    for r in range(row_blocks):
        diag = diag_ref[pl.ds(first_row + r, 1), :]
        for c in range(col_blocks):
            n = r * col_blocks + c
            one, two = (up_a_ref, down_a_ref) if n < half else (up_b_ref, down_b_ref)
            total = own_ref[n].astype(F32) + one[n % half].astype(F32) + two[n % half].astype(F32)
            on = jnp.logical_and(eye, first_row + r == first_col + c)
            total = total + jnp.where(on, jnp.broadcast_to(diag, (bs, bs)), 0.0)
            out_ref[r * bs:(r + 1) * bs, c * bs:(c + 1) * bs] = total


def on_device(factor_inv, pattern, border, row_scale, link_ids, first_diag):
    local_scen, rows, _ = factor_inv.shape
    nblk = pattern.shape[1]
    bs = border.shape[2]
    groups = link_ids.shape[1]
    tile = lax.axis_index(("x", "core"))
    z = lax.axis_index("z")
    y = lax.axis_index("y")
    y_count = lax.axis_size("y")
    order_blocks = first_diag.shape[0] // bs
    group_blocks = order_blocks // groups
    own_cols = group_blocks // y_count
    bins_y = group_blocks * own_cols

    borders = lax.all_to_all(border, ("x", "core"), 0, 0, tiled=True)

    masked = pl.pallas_call(
        mask_kernel,
        out_shape=jax.ShapeDtypeStruct((rows, rows), BF),
        in_specs=[SMEM, SMEM, HBM],
        out_specs=VMEM,
        scratch_shapes=[pltpu.VMEM((rows, rows), BF), pltpu.SemaphoreType.DMA((nblk,))],
        compiler_params=PARAMS,
        name="mask",
    )(tile.reshape(1), pattern.reshape(local_scen, nblk * nblk), factor_inv)
    scale = lax.dynamic_slice_in_dim(row_scale, tile, 1, 0).reshape(rows, 1)
    z_count = lax.axis_size("z")
    links = link_ids[None]
    step = 1
    while step < z_count:
        moved = lax.ppermute(links, "z", [(i, (i + step) % z_count) for i in range(z_count)])
        links = jnp.concatenate([links, moved])
        step *= 2
    links = links[(z - jnp.arange(z_count)) % z_count]
    row_bin = lax.dynamic_slice_in_dim(links, tile, 1, 2)[:, :, 0] - tile * group_blocks
    col_bin = lax.dynamic_slice_in_dim(links, z, 1, 2)[:, :, 0] - z * group_blocks
    target = (col_bin // own_cols) * bins_y + row_bin * own_cols + col_bin % own_cols
    target = target.T.reshape(-1)
    borders, masked, scale, target = lax.optimization_barrier((borders, masked, scale, target))
    pairs = pl.pallas_call(
        pair_kernel,
        out_shape=jax.ShapeDtypeStruct((groups * groups, bs, bs), BF),
        in_specs=[VMEM, VMEM, VMEM],
        out_specs=VMEM,
        scratch_shapes=[pltpu.VMEM((rows, groups * bs), BF) for _ in range(2)],
        compiler_params=PARAMS,
        name="pair",
    )(masked, borders, scale)
    received = lax.all_to_all(pairs, ("x", "core", "z"), 0, 0, tiled=True)
    half = jax.ShapeDtypeStruct((bins_y // 2, bs, bs), BF)
    own, far_a, far_b, up_b, down_a, up_a, down_b = pl.pallas_call(
        bin_kernel,
        out_shape=[jax.ShapeDtypeStruct((bins_y, bs, bs), BF)] + [half] * 6,
        in_specs=[SMEM, SMEM, VMEM],
        out_specs=[VMEM] * 7,
        scratch_shapes=[
            pltpu.VMEM((y_count * bins_y, bs, bs), F32),
        ],
        compiler_params=PARAMS,
        name="bins",
    )(y.reshape(1), target, received)
    def send(value, hop):
        return lax.ppermute(value, "y", [(k, (k + hop) % y_count) for k in range(y_count)])

    def add(one, two):
        return (one.astype(F32) + two.astype(F32)).astype(BF)

    far_a, far_b = send(far_a, 1), send(far_b, -1)
    up_b, down_a = send(up_b, 1), send(down_a, -1)
    up_a, down_b = send(add(up_a, far_a), 1), send(add(down_b, far_b), -1)
    place = jnp.stack([tile * group_blocks, z * group_blocks + y * own_cols])
    return pl.pallas_call(
        final_kernel,
        out_shape=jax.ShapeDtypeStruct((group_blocks * bs, own_cols * bs), F32),
        in_specs=[SMEM] + [VMEM] * 6,
        out_specs=VMEM,
        compiler_params=PARAMS,
        name="final",
    )(place, first_diag.reshape(order_blocks, bs), own, up_a, down_a, up_b, down_b)


def solution(mesh):
    chips = Mesh(mesh.devices.reshape(8, 4, 4, 2), ("z", "y", "x", "core"))
    scen, tile = ("z", "y"), ("x", "core")
    in_specs = (
        P(scen, None, None),
        P(scen, None, None),
        P(scen, None, tile),
        P(scen, None),
        P(scen, None),
        P(),
    )
    return jax.shard_map(
        on_device, mesh=chips, in_specs=in_specs, out_specs=P(tile, scen), check_vma=False
    )
```

```python
import jax
import jax.numpy as jnp
from jax import lax
from jax.experimental import pallas as pl
from jax.experimental.pallas import tpu as pltpu
from jax.sharding import Mesh, PartitionSpec as P

BF = jnp.bfloat16
F32 = jnp.float32

VMEM = pl.BlockSpec(memory_space=pltpu.VMEM)
SMEM = pl.BlockSpec(memory_space=pltpu.SMEM)
HBM = pl.BlockSpec(memory_space=pltpu.HBM)
PARAMS = pltpu.CompilerParams(vmem_limit_bytes=32 << 20)


def mask_kernel(tile_ref, pattern_ref, factor_hbm, out_ref, buf_ref, sems):
    rows = buf_ref.shape[0]
    nblk = sems.shape[0]
    bs = rows // nblk
    tile = tile_ref[0]
    copies = [
        pltpu.make_async_copy(
            factor_hbm.at[tile, pl.ds(a * bs, bs), :], buf_ref.at[pl.ds(a * bs, bs), :], sems.at[a]
        )
        for a in range(nblk)
    ]
    for copy in copies:
        copy.start()
    for a in range(nblk):
        copies[a].wait()
        lo, hi = a * bs, (a + 1) * bs
        for b in range(nblk):
            block = buf_ref[lo:hi, b * bs:(b + 1) * bs]
            if b < a:
                keep = pattern_ref[tile, a * nblk + b] != 0
                block = jnp.where(keep, block, jnp.zeros_like(block))
            if b > a:
                block = jnp.zeros_like(block)
            out_ref[lo:hi, b * bs:(b + 1) * bs] = block


def pair_kernel(masked_ref, border_ref, scale_ref, out_ref, solved_ref, scaled_ref):
    groups, rows, bs = border_ref.shape
    for g in range(0, groups, 2):
        rhs = jnp.concatenate([border_ref[g], border_ref[g + 1]], axis=1)
        for a in range(0, rows, 2 * bs):
            lo, hi = a, a + 2 * bs
            solved = jnp.dot(
                masked_ref[lo:hi, :hi], rhs[:hi], preferred_element_type=F32
            ).astype(BF)
            solved_ref[lo:hi, g * bs:(g + 2) * bs] = solved
            scaled_ref[lo:hi, g * bs:(g + 2) * bs] = (
                scale_ref[lo:hi, :] * solved.astype(F32)
            ).astype(BF)
    for i in range(0, groups, 2):
        lhs = scaled_ref[:, i * bs:(i + 2) * bs]
        for j in range(0, groups, 2):
            rhs = solved_ref[:, j * bs:(j + 2) * bs]
            pair = lax.dot_general(
                lhs, rhs, (((0,), (0,)), ((), ())), preferred_element_type=F32
            ).astype(BF)
            for di in range(2):
                for dj in range(2):
                    out_ref[(i + di) * groups + j + dj] = pair[
                        di * bs:(di + 1) * bs, dj * bs:(dj + 1) * bs
                    ]


def bin_kernel(shift_ref, target_ref, in_ref, *rest):
    own, far_a, far_b, up_b, down_a, up_a, down_b = rest[:7]
    acc_ref = rest[7]
    acc_ref[...] = jnp.zeros_like(acc_ref)
    for k in range(in_ref.shape[0]):
        acc_ref[target_ref[k]] += in_ref[k].astype(F32)
    per = own.shape[0]
    parts = acc_ref.shape[0] // per
    for hop, pieces in ((2, (far_a, far_b)), (1, (up_a, up_b)), (3, (down_a, down_b)), (0, (own,))):
        start = lax.rem(shift_ref[0] + hop, parts) * per
        size = per // len(pieces)
        for n, piece in enumerate(pieces):
            piece[...] = acc_ref[pl.ds(start + n * size, size)].astype(BF)


def final_kernel(where_ref, diag_ref, own_ref, up_a_ref, down_a_ref, up_b_ref, down_b_ref, out_ref):
    count, bs, _ = own_ref.shape
    row_blocks = out_ref.shape[0] // bs
    col_blocks = out_ref.shape[1] // bs
    half = count // 2
    first_row = where_ref[0]
    first_col = where_ref[1]
    eye = lax.broadcasted_iota(jnp.int32, (bs, bs), 0) == lax.broadcasted_iota(jnp.int32, (bs, bs), 1)
    for r in range(row_blocks):
        diag = diag_ref[pl.ds(first_row + r, 1), :]
        for c in range(col_blocks):
            n = r * col_blocks + c
            one, two = (up_a_ref, down_a_ref) if n < half else (up_b_ref, down_b_ref)
            total = own_ref[n].astype(F32) + one[n % half].astype(F32) + two[n % half].astype(F32)
            on = jnp.logical_and(eye, first_row + r == first_col + c)
            total = total + jnp.where(on, jnp.broadcast_to(diag, (bs, bs)), 0.0)
            out_ref[r * bs:(r + 1) * bs, c * bs:(c + 1) * bs] = total


def on_device(factor_inv, pattern, border, row_scale, link_ids, first_diag):
    local_scen, rows, _ = factor_inv.shape
    nblk = pattern.shape[1]
    bs = border.shape[2]
    groups = link_ids.shape[1]
    tile = lax.axis_index(("x", "core"))
    z = lax.axis_index("z")
    y = lax.axis_index("y")
    y_count = lax.axis_size("y")
    order_blocks = first_diag.shape[0] // bs
    group_blocks = order_blocks // groups
    own_cols = group_blocks // y_count
    bins_y = group_blocks * own_cols

    borders = lax.all_to_all(border, ("x", "core"), 0, 0, tiled=True)

    masked = pl.pallas_call(
        mask_kernel,
        out_shape=jax.ShapeDtypeStruct((rows, rows), BF),
        in_specs=[SMEM, SMEM, HBM],
        out_specs=VMEM,
        scratch_shapes=[pltpu.VMEM((rows, rows), BF), pltpu.SemaphoreType.DMA((nblk,))],
        compiler_params=pltpu.CompilerParams(vmem_limit_bytes=48 << 20),
        name="mask",
    )(tile.reshape(1), pattern.reshape(local_scen, nblk * nblk), factor_inv)
    scale = lax.dynamic_slice_in_dim(row_scale, tile, 1, 0).reshape(rows, 1)
    z_count = lax.axis_size("z")
    links = link_ids[None]
    step = 1
    while step < z_count:
        moved = lax.ppermute(links, "z", [(i, (i + step) % z_count) for i in range(z_count)])
        links = jnp.concatenate([links, moved])
        step *= 2
    links = links[(z - jnp.arange(z_count)) % z_count]
    row_bin = lax.dynamic_slice_in_dim(links, tile, 1, 2)[:, :, 0] - tile * group_blocks
    col_bin = lax.dynamic_slice_in_dim(links, z, 1, 2)[:, :, 0] - z * group_blocks
    target = (col_bin // own_cols) * bins_y + row_bin * own_cols + col_bin % own_cols
    target = target.T.reshape(-1)
    borders, masked, scale, target = lax.optimization_barrier((borders, masked, scale, target))
    pairs = pl.pallas_call(
        pair_kernel,
        out_shape=jax.ShapeDtypeStruct((groups * groups, bs, bs), BF),
        in_specs=[VMEM, VMEM, VMEM],
        out_specs=VMEM,
        scratch_shapes=[pltpu.VMEM((rows, groups * bs), BF) for _ in range(2)],
        compiler_params=PARAMS,
        name="pair",
    )(masked, borders, scale)
    received = lax.all_to_all(pairs, ("x", "core", "z"), 0, 0, tiled=True)
    half = jax.ShapeDtypeStruct((bins_y // 2, bs, bs), BF)
    own, far_a, far_b, up_b, down_a, up_a, down_b = pl.pallas_call(
        bin_kernel,
        out_shape=[jax.ShapeDtypeStruct((bins_y, bs, bs), BF)] + [half] * 6,
        in_specs=[SMEM, SMEM, VMEM],
        out_specs=[VMEM] * 7,
        scratch_shapes=[
            pltpu.VMEM((y_count * bins_y, bs, bs), F32),
        ],
        compiler_params=PARAMS,
        name="bins",
    )(y.reshape(1), target, received)
    def send(value, hop):
        return lax.ppermute(value, "y", [(k, (k + hop) % y_count) for k in range(y_count)])

    def add(one, two):
        return (one.astype(F32) + two.astype(F32)).astype(BF)

    far_a, far_b = send(far_a, 1), send(far_b, -1)
    up_b, down_a = send(up_b, 1), send(down_a, -1)
    up_a, down_b = send(add(up_a, far_a), 1), send(add(down_b, far_b), -1)
    place = jnp.stack([tile * group_blocks, z * group_blocks + y * own_cols])
    return pl.pallas_call(
        final_kernel,
        out_shape=jax.ShapeDtypeStruct((group_blocks * bs, own_cols * bs), F32),
        in_specs=[SMEM] + [VMEM] * 6,
        out_specs=VMEM,
        compiler_params=PARAMS,
        name="final",
    )(place, first_diag.reshape(order_blocks, bs), own, up_a, down_a, up_b, down_b)


def solution(mesh):
    chips = Mesh(mesh.devices.reshape(8, 4, 4, 2), ("z", "y", "x", "core"))
    scen, tile = ("z", "y"), ("x", "core")
    in_specs = (
        P(scen, None, None),
        P(scen, None, None),
        P(scen, None, tile),
        P(scen, None),
        P(scen, None),
        P(),
    )
    return jax.shard_map(
        on_device, mesh=chips, in_specs=in_specs, out_specs=P(tile, scen), check_vma=False
    )
```
